32 devices in a mesh: tm: 8 (over z, core), space: 4 (over y, x).
Axes of the slice: x: 2, y: 2, z: 4, core: 2. Of those that a mesh axis runs over, the one named last changes fastest.
Arguments:
- snapshots: bfloat16 [4096, 12288], P('tm', 'space')
- freq_ids: int32 [64], replicated, may hold values from 0 to 127
Outputs:
- gram: float32 [64, 2, 15, 15], P('tm')
The draws below stay inside these ranges and needn't reach their ends.
All inputs are finite; a program needn't handle non-finite values.
Results may differ from the reference program's by a relative error of at most 0.00039.
Values may be sent and summed in bfloat16 or wider, within the bound.
No kernel may reach another device: no remote copies, remote signals or barrier semaphores. Data moves between devices by JAX's collectives and lax.ppermute only.
A program may use at most 64 MiB of HBM per device.

```python
import math
import jax
import jax.numpy as jnp
from jax import lax

NFFT = 512
F = 64
NB = 15
TIMES = 4096
PTS = 12288


def draw_snapshots(key, part):
    keys = jax.random.split(key, 5)
    noise = jax.random.normal(keys[0], (TIMES, PTS), jnp.float32)
    scales = jnp.exp(jax.random.uniform(keys[1], (PTS,), jnp.float32, math.log(0.5), math.log(2.0)))
    times = jnp.arange(TIMES, dtype=jnp.float32)
    bins = jax.random.uniform(keys[2], (12,), jnp.float32, 0.0, NFFT / 4.0)
    omegas = bins * (2.0 * math.pi / NFFT)
    amp_cos = 0.15 * jax.random.normal(keys[3], (12, PTS), jnp.float32)
    sine_amplitude = 0.15 * jax.random.normal(keys[4], (12, PTS), jnp.float32)
    field = noise
    for index in range(12):
        phase = omegas[index] * times
        field = field + jnp.cos(phase)[:, None] * amp_cos[index][None, :] + jnp.sin(phase)[:, None] * sine_amplitude[index][None, :]
    return (field * scales[None, :]).astype(jnp.bfloat16)


def touch_ends(drawn, stream_key, low, largest):
    extent = drawn.shape
    place = [jax.random.randint(jax.random.fold_in(stream_key, axis), (), 0, extent[axis]) for axis in range(len(extent))]
    drawn = drawn.at[tuple(place)].set(low)
    longest = extent.index(max(extent))
    place[longest] = (place[longest] + 1) % extent[longest]
    return drawn.at[tuple(place)].set(largest)


def setup_inputs(seed: int = 0) -> dict:
    streams_of = jax.random.split(jax.random.key(seed), 3)
    return {
        "snapshots": draw_snapshots(jax.random.fold_in(streams_of[2], 71), 0),
        "freq_ids": touch_ends(jax.random.randint(streams_of[1], (F,), 0, NFFT // 4), jax.random.fold_in(streams_of[1], 1), 0, (NFFT // 4) - 1).astype(jnp.int32),
    }


def kernel_values(freqs, shifts, window_length):
    phase = (freqs * shifts) % window_length
    angle = (2.0 * math.pi / window_length) * phase.astype(jnp.float32)
    window = 0.5 - 0.5 * jnp.cos((2.0 * math.pi / window_length) * shifts.astype(jnp.float32))
    return window * jnp.cos(angle), -window * jnp.sin(angle)


def reference(snapshots, freq_ids):
    shifts = jnp.arange(NFFT, dtype=jnp.int32)
    real_part, imag_part = kernel_values(freq_ids[:, None], shifts[None, :], NFFT)
    table = jnp.stack([real_part, imag_part], axis=1).reshape(2 * F, NFFT).astype(jnp.bfloat16)
    starts = (jnp.arange(NB, dtype=jnp.int32) * (NFFT // 2)).astype(jnp.int32)

    def one_block(start):
        segment = lax.dynamic_slice_in_dim(snapshots, start, NFFT, 0)
        return jnp.dot(table, segment, preferred_element_type=jnp.float32).astype(jnp.bfloat16)

    blockdft = lax.map(one_block, starts)
    scale = 1.0 / (NFFT * PTS)

    def one_freq(index):
        pair = lax.dynamic_slice_in_dim(blockdft, (2 * index).astype(jnp.int32), 2, 1)
        stacked_snapshot_rows = jnp.concatenate([pair[:, 0, :], pair[:, 1, :]], axis=0)
        cross_product_terms = jnp.dot(stacked_snapshot_rows, stacked_snapshot_rows.T, preferred_element_type=jnp.float32)
        gram_real_matrix = cross_product_terms[:NB, :NB] + cross_product_terms[NB:, NB:]
        imag_gram = cross_product_terms[NB:, :NB] - cross_product_terms[:NB, NB:]
        return jnp.stack([gram_real_matrix, imag_gram], axis=0) * scale

    return lax.map(one_freq, jnp.arange(F, dtype=jnp.int32))
```

```python
import functools
import math

import jax
import jax.numpy as jnp
from jax import lax
from jax.experimental import pallas as pl
from jax.experimental.pallas import tpu as pltpu
from jax.sharding import PartitionSpec as P

NFFT = 512


def point_block(points, limit):
    block = min(points, limit)
    while points % block or block % 128:
        block -= 128
    return block


def call(body, grid, in_specs, out_specs, out_shape, scratch=(), flops=0, moved=0):
    return pl.pallas_call(
        body,
        grid=grid,
        in_specs=in_specs,
        out_specs=out_specs,
        out_shape=out_shape,
        scratch_shapes=scratch,
        cost_estimate=pl.CostEstimate(flops=flops, bytes_accessed=moved, transcendentals=0),
    )


def stack_spec(lead, rows, block):
    zeros = (0,) * (len(lead) + 1)
    return pl.BlockSpec((*lead, rows, block), lambda i: (*zeros, i))


def bf16(*shape):
    return jax.ShapeDtypeStruct(shape, jnp.bfloat16)


def half_table(freq_ids, chips, core):
    hop = NFFT // 2
    per_owner = freq_ids.shape[0] // (2 * chips)
    pairs = freq_ids.reshape(chips, 2, per_owner)
    own = jnp.where(core == 0, pairs[:, 0], pairs[:, 1])
    other = jnp.where(core == 0, pairs[:, 1], pairs[:, 0])
    freqs = jnp.stack([own, other])[None, :, :, None, :, None]
    shape = (2, 2, chips, 2, per_owner, hop)
    shifts = lax.broadcasted_iota(jnp.int32, shape, 5) + hop * lax.broadcasted_iota(jnp.int32, shape, 0)
    quarter = (NFFT // 4) * lax.broadcasted_iota(jnp.int32, shape, 3)
    step = 2.0 * math.pi / NFFT
    angle = step * ((freqs * shifts + quarter) % NFFT).astype(jnp.float32)
    window = 0.5 - 0.5 * jnp.cos(step * shifts.astype(jnp.float32))
    return (window * jnp.cos(angle)).astype(jnp.bfloat16).reshape(-1, hop)


def transform_body(chips, rows, table_ref, snap_ref, own_ref, other_ref):
    hop = table_ref.shape[1]
    half = table_ref.shape[0] // 2
    table = table_ref[...]
    early = jnp.dot(table, snap_ref[:hop, :], preferred_element_type=jnp.float32)
    late = jnp.dot(table, snap_ref[hop:, :], preferred_element_type=jnp.float32)
    units = (early[:half] + late[half:], early[half:], late[:half])
    for u, unit in enumerate(units):
        unit = unit.astype(jnp.bfloat16)
        for y in range(chips):
            own_ref[u, y] = unit[y * rows : (y + 1) * rows]
            other_ref[u, y] = unit[half // 2 + y * rows : half // 2 + (y + 1) * rows]


def add(a, b):
    return (a.astype(jnp.float32) + b.astype(jnp.float32)).astype(jnp.bfloat16)


def spread_body(chips, own_ref, got_ref, near_ref, loc_ref, keep_ref, *main_refs):
    device = lax.axis_index("tm")
    chip, core = device // 2, device % 2

    def write(low, high):
        def five(owner, ref):
            ref[0] = low[0, owner]
            ref[1] = add(low[2, owner], high[1, owner])
            ref[2] = high[0, owner]
            if ref.shape[0] > 3:
                ref[3] = low[1, owner]
                ref[4] = high[2, owner]

        five(chip, loc_ref)
        five(chip ^ 1, near_ref)
        for s in range(2, chips):
            owner = chip ^ s
            five(owner, main_refs[s - 2])
            even = chip % 2 == 0
            toward = jnp.where(even, high[2, owner], low[1, owner])
            keep_ref[0, s - 2] = toward
            keep_ref[1, s - 2] = jnp.where(even, low[1, owner], high[2, owner])
            owner = chip ^ 1 ^ s
            near_ref[3 + s] = jnp.where(even, high[2, owner], low[1, owner])

    @pl.when(core == 0)
    def _():
        write(own_ref, got_ref)

    @pl.when(core == 1)
    def _():
        write(got_ref, own_ref)


def merge_body(chips, keep_ref, near_ref, *out_refs):
    for s in range(2, chips):
        out_refs[s - 2][0] = add(keep_ref[0, s - 2], near_ref[3 + s])
        out_refs[s - 2][1] = keep_ref[1, s - 2]


def gram_body(chips, scale, loc_ref, near_ref, *refs):
    count = chips - 2
    mains, extras, thirds = refs[:count], refs[count : 2 * count], refs[2 * count : -3]
    out_ref, data, total = refs[-3:]
    slots, rows, block = data.shape
    step = pl.program_id(0)
    chip = lax.axis_index("tm") // 2

    def accumulate(slot, value):
        slot = lax.rem(slot + slots, slots)
        data[slot] = add(data[slot], value)

    def place(y, ref):
        for j in range(3):
            data[4 * y + j] = ref[j]

    for y in range(chips):
        data[4 * y + 3] = jnp.zeros((rows, block), jnp.bfloat16)
    place(chip, loc_ref)
    place(chip ^ 1, near_ref)
    for y, ref in ((chip, loc_ref), (chip ^ 1, near_ref)):
        accumulate(4 * y - 1, ref[3])
        accumulate(4 * y + 3, ref[4])
    for s in range(2, chips):
        y = chip ^ s
        odd = y % 2 == 1
        away = jnp.where(odd, 4 * y + 3, 4 * y - 1)
        place(y, mains[s - 2])

        @pl.when(odd == (chip > y))
        def _():
            accumulate(4 * (y - y % 2) + 3, extras[s - 2][0])
            accumulate(away, extras[s - 2][1])

        if thirds:

            @pl.when(odd != (chip > y))
            def _():
                accumulate(away, thirds[s - 2][0])

    whole = data[...].reshape(slots * rows, block)
    product = lax.dot_general(whole, whole, (((1,), (1,)), ((), ())), preferred_element_type=jnp.float32)

    @pl.when(step == 0)
    def _():
        total[...] = product

    @pl.when(step > 0)
    def _():
        total[...] += product

    @pl.when(step == pl.num_programs(0) - 1)
    def _():
        per = rows // 2
        size = slots * rows
        same = lax.broadcasted_iota(jnp.int32, (size, size), 0) % per == lax.broadcasted_iota(
            jnp.int32, (size, size), 1
        ) % per
        picked = jnp.where(same, total[...], 0.0).reshape(slots, 2, per, size).sum(axis=2)
        real, imag = picked[:, 0], picked[:, 1]
        second = (lax.broadcasted_iota(jnp.int32, (slots, size), 1) // per) % 2 == 1
        diagonal = real + pltpu.roll(imag, size - per, 1)
        crossed = pltpu.roll(imag, per, 1) - real
        out_ref[...] = jnp.where(second, crossed, diagonal) * scale


def reduce_space(value):
    count = lax.axis_size("space")
    stride = 1
    while stride < count:
        step = 4 if stride * 4 <= count else 2
        parts = [value] + [
            lax.ppermute(value, "space", [(i, i ^ (stride * s)) for i in range(count)]) for s in range(1, step)
        ]
        while len(parts) > 1:
            parts = [a + b for a, b in zip(parts[::2], parts[1::2])]
        value = parts[0]
        stride *= step
    return value


def local(snapshots, freq_ids):
    hop = NFFT // 2
    devices = lax.axis_size("tm")
    chips = devices // 2
    blocks = 2 * devices - 1
    slots = 2 * devices
    points = snapshots.shape[1]
    per_owner = freq_ids.shape[0] // devices
    rows = 2 * per_owner
    core = lax.axis_index("tm") % 2

    def across(value, s, keep=lambda y: True):
        route = [(2 * y + c, 2 * (y ^ s) + c) for y in range(chips) for c in range(2) if keep(y)]
        return lax.ppermute(value, "tm", route)

    table = half_table(freq_ids, chips, core)
    block = point_block(points, 1024)
    grid = (points // block,)
    size = table.shape[0] * points
    own, other = call(
        functools.partial(transform_body, chips, rows),
        grid,
        [pl.BlockSpec(table.shape, lambda i: (0, 0)), pl.BlockSpec((NFFT, block), lambda i: (0, i))],
        [stack_spec((3, chips), rows, block)] * 2,
        [bf16(3, chips, rows, points)] * 2,
        flops=4 * size * hop,
        moved=5 * size,
    )(table, snapshots)
    got = lax.ppermute(other, "tm", [(i, i ^ 1) for i in range(devices)])
    far = chips - 2
    near, loc, keep, *mains = call(
        functools.partial(spread_body, chips),
        grid,
        [stack_spec((3, chips), rows, block)] * 2,
        [
            stack_spec((5 + far,), rows, block),
            stack_spec((5,), rows, block),
            stack_spec((2, far), rows, block),
            *([stack_spec((3,), rows, block)] * far),
        ],
        [
            bf16(5 + far, rows, points),
            bf16(5, rows, points),
            bf16(2, far, rows, points),
            *([bf16(3, rows, points)] * far),
        ],
        moved=5 * size,
    )(own, got)
    near = across(near, 1)
    mains = [across(mains[s - 2], s) for s in range(2, chips)]
    extras = call(
        functools.partial(merge_body, chips),
        grid,
        [stack_spec((2, far), rows, block), stack_spec((5 + far,), rows, block)],
        [stack_spec((2,), rows, block)] * far,
        [bf16(2, rows, points)] * far,
        moved=2 * size,
    )(keep, near)

    def outward(s):
        return lambda y: (y % 2 == 1) == ((y ^ s) > y)

    def third(s):
        return lambda y: (y % 2 == 1) != ((y ^ s) > y) and y not in (0, chips - 1)

    thirds = []
    if chips > 4:
        thirds = [across(keep[1:, s - 2], s, third(s)) for s in range(2, chips)]
    extras = [across(extras[s - 2], s, outward(s)) for s in range(2, chips)]
    scale = 1.0 / (NFFT * points * lax.axis_size("space"))
    total = slots * rows
    reduced = call(
        functools.partial(gram_body, chips, scale),
        grid,
        [stack_spec((5,), rows, block), stack_spec((5 + far,), rows, block)]
        + [stack_spec((3,), rows, block)] * far
        + [stack_spec((2,), rows, block)] * far
        + [stack_spec((1,), rows, block)] * len(thirds),
        pl.BlockSpec((slots, total), lambda i: (0, 0)),
        jax.ShapeDtypeStruct((slots, total), jnp.float32),
        [pltpu.VMEM((slots, rows, block), jnp.bfloat16), pltpu.VMEM((total, total), jnp.float32)],
        flops=2 * total * total * points,
        moved=2 * total * points,
    )(loc, near, *mains, *extras, *thirds)
    reduced = reduce_space(reduced)
    parts = reduced.reshape(slots, slots, 2, per_owner)[:blocks, :blocks]
    return jnp.transpose(parts, (3, 2, 0, 1))


def solution(mesh):
    return jax.shard_map(
        local,
        mesh=mesh,
        in_specs=(P("tm", "space"), P()),
        out_specs=P("tm", None, None, None),
        check_vma=False,
    )
```

```python
import functools
import math

import jax
import jax.numpy as jnp
from jax import lax
from jax.experimental import pallas as pl
from jax.experimental.pallas import tpu as pltpu
from jax.sharding import PartitionSpec as P


NFFT = 512
HOP = NFFT // 2


ON_CHIP = pl.BlockSpec(memory_space=pltpu.VMEM)
IN_PLACE = pl.BlockSpec(memory_space=pltpu.HBM)


def bf16(*shape):
    return jax.ShapeDtypeStruct(shape, jnp.bfloat16)


def call(body, args, out_shape, in_specs=None, scratch=(), flops=0, moved=0, grant=24):
    return pl.pallas_call(
        body,
        in_specs=in_specs or [ON_CHIP] * len(args),
        out_specs=jax.tree.map(lambda _: ON_CHIP, out_shape),
        out_shape=out_shape,
        scratch_shapes=scratch,
        cost_estimate=pl.CostEstimate(flops=flops, bytes_accessed=moved, transcendentals=0),
        compiler_params=pltpu.CompilerParams(vmem_limit_bytes=grant << 20),
    )(*args)


def add(a, b):
    return (a.astype(jnp.float32) + b.astype(jnp.float32)).astype(jnp.bfloat16)


def cosine(phase):
    quarter = jnp.abs(phase - NFFT // 2) - NFFT // 4
    x = quarter.astype(jnp.float32) * (2.0 * math.pi / NFFT)
    square = x * x
    value = jnp.full_like(x, 1.0 / math.factorial(13))
    for order in (11, 9, 7, 5, 3, 1):
        value = value * square + (-1.0) ** (order // 2) / math.factorial(order)
    return value * x


def half_tables(freq_ref, chips, per_owner, chip, core):
    count = freq_ref.shape[1]
    row = lax.broadcasted_iota(jnp.int32, (2 * count, count), 0)
    lane = lax.broadcasted_iota(jnp.int32, (2 * count, count), 1)
    rows = 2 * per_owner
    away = (row // rows) % chips
    owner = 2 * (away ^ chip) + ((row // (rows * chips)) ^ core)
    picked = jnp.where(lane == owner * per_owner + row % per_owner, freq_ref[...], 0)
    freq = jnp.sum(picked.astype(jnp.float32), axis=1, keepdims=True).astype(jnp.int32)
    shape = (2 * count, HOP)
    part = (lax.broadcasted_iota(jnp.int32, shape, 0) // per_owner) % 2
    shift = lax.broadcasted_iota(jnp.int32, shape, 1)
    wave = cosine((freq * shift + part * (NFFT // 4)) & (NFFT - 1))
    taper = 0.5 * cosine(lax.broadcasted_iota(jnp.int32, (8, HOP), 1))[:1]
    sign = (1 - 2 * (freq & 1)).astype(jnp.float32)
    early = ((0.5 - taper) * wave).astype(jnp.bfloat16)
    late = ((0.5 + taper) * (wave * sign)).astype(jnp.bfloat16)
    return early, late


def transform_body(chips, rows, freq_ref, snap_ref, own_ref, other_ref, *refs):
    far_refs, (stage, sems) = refs[:-2], refs[-2:]
    device = lax.axis_index("tm")
    points = snap_ref.shape[1]
    pieces = sems.shape[0]
    block = points // pieces
    copies = [
        pltpu.make_async_copy(
            snap_ref.at[:, pl.ds(i * block, block)], stage.at[:, pl.ds(i * block, block)], sems.at[i]
        )
        for i in range(pieces)
    ]
    for copy in copies:
        copy.start()
    early, late = half_tables(freq_ref, chips, rows // 2, device // 2, device % 2)
    table = jnp.concatenate([early, late], axis=0)
    half = early.shape[0]
    for i, copy in enumerate(copies):
        copy.wait()
        columns = pl.ds(i * block, block)
        first = jnp.dot(table, stage[:HOP, columns], preferred_element_type=jnp.float32)
        second = jnp.dot(table, stage[HOP:, columns], preferred_element_type=jnp.float32)
        units = (first[:half] + second[half:], first[half:], second[:half])
        for u, unit in enumerate(units):
            unit = unit.astype(jnp.bfloat16)
            for s in range(chips):
                value = unit[s * rows : (s + 1) * rows]
                if u == 0 and s >= 2:
                    far_refs[s - 2][:, columns] = value
                else:
                    own_ref[u, s, :, columns] = value
                other_ref[u, s, :, columns] = unit[half // 2 + s * rows : half // 2 + (s + 1) * rows]


def spread_body(chips, own_ref, got_ref, halo_ref, near_ref, loc_ref, keep_ref, *main_refs):
    device = lax.axis_index("tm")
    chip, core = device // 2, device % 2

    def write(low, high):
        for s, ref in ((0, loc_ref), (1, near_ref)):
            ref[0] = low[0, s]
            ref[1] = add(low[2, s], high[1, s])
            ref[2] = high[0, s]
            ref[3] = low[1, s]
            ref[4] = high[2, s]
        for s in range(2, chips):
            main_refs[s - 2][0] = add(low[2, s], high[1, s])
            main_refs[s - 2][1] = got_ref[0, s]

        def outer(toward, away):
            for s in range(2, chips):
                halo_ref[s - 2] = toward(s ^ 1)
                keep_ref[0, s - 2] = toward(s)
                keep_ref[1, s - 2] = away(s)

        @pl.when(chip % 2 == 0)
        def _():
            outer(lambda s: high[2, s], lambda s: low[1, s])

        @pl.when(chip % 2 == 1)
        def _():
            outer(lambda s: low[1, s], lambda s: high[2, s])

    @pl.when(core == 0)
    def _():
        write(own_ref, got_ref)

    @pl.when(core == 1)
    def _():
        write(got_ref, own_ref)


def merge_body(chips, keep_ref, halo_ref, *out_refs):
    for s in range(2, chips):
        out_refs[s - 2][0] = add(keep_ref[0, s - 2], halo_ref[s - 2])
        out_refs[s - 2][1] = keep_ref[1, s - 2]


def gram_body(chips, scale, loc_ref, near_ref, *refs):
    count = chips - 2
    owns, mains, extras = refs[:count], refs[count : 2 * count], refs[2 * count : 3 * count]
    thirds = refs[3 * count : -2]
    out_ref, data = refs[-2:]
    slots, rows, points = data.shape
    device = lax.axis_index("tm")
    chip, core = device // 2, device % 2

    def accumulate(slot, value):
        slot = lax.rem(slot + slots, slots)
        data[slot] = add(data[slot], value)

    for y in range(chips):
        data[4 * y + 3] = jnp.zeros((rows, points), jnp.bfloat16)
    for y, ref in ((chip, loc_ref), (chip ^ 1, near_ref)):
        for j in range(3):
            data[4 * y + j] = ref[j]
        accumulate(4 * y - 1, ref[3])
        accumulate(4 * y + 3, ref[4])
    for s in range(2, chips):
        y = chip ^ s
        odd = y % 2 == 1
        away = jnp.where(odd, 4 * y + 3, 4 * y - 1)
        data[4 * y + 2 * core] = owns[s - 2][...]
        data[4 * y + 1] = mains[s - 2][0]
        data[4 * y + 2 - 2 * core] = mains[s - 2][1]

        @pl.when(odd == (chip > y))
        def _():
            accumulate(4 * (y - y % 2) + 3, extras[s - 2][0])
            accumulate(away, extras[s - 2][1])

        if thirds:

            @pl.when(odd != (chip > y))
            def _():
                accumulate(away, thirds[s - 2][0])

    whole = data[...].reshape(slots * rows, points)
    total = lax.dot_general(whole, whole, (((1,), (1,)), ((), ())), preferred_element_type=jnp.float32)
    per = rows // 2
    size = slots * rows
    row = lax.broadcasted_iota(jnp.int32, (size, size), 0)
    lane = lax.broadcasted_iota(jnp.int32, (size, size), 1)
    picked = jnp.where(row % per == lane % per, total, 0.0).reshape(slots, 2, per, size).sum(axis=2)
    real, imag = picked[:, 0], picked[:, 1]
    second = (lax.broadcasted_iota(jnp.int32, (slots, size), 1) // per) % 2 == 1
    diagonal = real + pltpu.roll(imag, size - per, 1)
    crossed = pltpu.roll(imag, per, 1) - real
    out_ref[...] = jnp.where(second, crossed, diagonal) * scale


def reduce_space(value):
    count = lax.axis_size("space")
    stride = 1
    while stride < count:
        step = 4 if stride * 4 <= count else 2
        parts = [value] + [
            lax.ppermute(value, "space", [(i, i ^ (stride * s)) for i in range(count)]) for s in range(1, step)
        ]
        while len(parts) > 1:
            parts = [a + b for a, b in zip(parts[::2], parts[1::2])]
        value = parts[0]
        stride *= step
    return value


def local(snapshots, freq_ids):
    devices = lax.axis_size("tm")
    chips = devices // 2
    far = range(2, chips)
    count = chips - 2
    blocks = 2 * devices - 1
    slots = 2 * devices
    points = snapshots.shape[1]
    per_owner = freq_ids.shape[0] // devices
    rows = 2 * per_owner

    def across(value, s, keep=lambda y: True):
        route = [(2 * y + c, 2 * (y ^ s) + c) for y in range(chips) for c in range(2) if keep(y)]
        return lax.ppermute(value, "tm", route)

    def outward(s):
        return lambda y: (y % 2 == 1) == ((y ^ s) > y)

    def third(s):
        return lambda y: (y % 2 == 1) != ((y ^ s) > y) and y not in (0, chips - 1)

    size = 4 * freq_ids.shape[0] * points
    pieces = 6 if points % 768 == 0 else 1
    own, other, *owns = call(
        functools.partial(transform_body, chips, rows),
        (freq_ids.reshape(1, -1), snapshots),
        [bf16(3, chips, rows, points)] * 2 + [bf16(rows, points)] * count,
        [ON_CHIP, IN_PLACE],
        [pltpu.VMEM((NFFT, points), jnp.bfloat16), pltpu.SemaphoreType.DMA((pieces,))],
        flops=4 * size * HOP,
        moved=5 * size,
        grant=24,
    )
    got = lax.ppermute(other, "tm", [(i, i ^ 1) for i in range(devices)])
    owns = [across(owns[s - 2], s) for s in far]
    halo, near, loc, keep, *mains = call(
        functools.partial(spread_body, chips),
        (own, got),
        [
            bf16(count, rows, points),
            bf16(5, rows, points),
            bf16(5, rows, points),
            bf16(2, count, rows, points),
            *([bf16(2, rows, points)] * count),
        ],
        moved=5 * size,
    )
    halo = across(halo, 1, lambda y: chips > 4 or y in (0, chips - 1))
    near = across(near, 1)
    mains = [across(mains[s - 2], s) for s in far]
    extras = call(
        functools.partial(merge_body, chips),
        (keep, halo),
        [bf16(2, rows, points)] * count,
        moved=2 * size,
    )
    thirds = []
    if chips > 4:
        thirds = [across(keep[1:, s - 2], s, third(s)) for s in far]
    extras = [across(extras[s - 2], s, outward(s)) for s in far]
    scale = 1.0 / (NFFT * points * lax.axis_size("space"))
    total = slots * rows
    reduced = call(
        functools.partial(gram_body, chips, scale),
        (loc, near, *owns, *mains, *extras, *thirds),
        jax.ShapeDtypeStruct((slots, total), jnp.float32),
        None,
        [pltpu.VMEM((slots, rows, points), jnp.bfloat16)],
        flops=2 * total * total * points,
        moved=2 * total * points,
    )
    reduced = reduce_space(reduced)
    parts = reduced.reshape(slots, slots, 2, per_owner)[:blocks, :blocks]
    return jnp.transpose(parts, (3, 2, 0, 1))


def solution(mesh):
    return jax.shard_map(
        local,
        mesh=mesh,
        in_specs=(P("tm", "space"), P()),
        out_specs=P("tm", None, None, None),
        check_vma=False,
    )
```
